32 devices in a mesh: dp: 32 (over z, y, x, core).
Axes of the slice: x: 2, y: 2, z: 4, core: 2. Of those that a mesh axis runs over, the one named last changes fastest.
Arguments:
- hidden_in: bfloat16 [4096, 640], P('dp'), may hold values from -6 to 6
- cotangent: bfloat16 [4096, 640], P('dp'), may hold values from -6 to 6
- params: float32 [5573632], P('dp'), may hold values from -4 to 4
- moment_one: float32 [5573632], P('dp'), may hold values from -6 to 6
- moment_two: float32 [5573632], P('dp'), may hold values from 0.02 to 0.5
- seq_lengths: int32 [64], replicated, may hold values from 0 to 128, as said below
- seq_owner: int32 [64], replicated, may hold values from 0 to 31, as said below
Outputs:
- block_out: bfloat16 [4096, 640], P('dp')
- grad_in: float32 [4096, 640], P('dp')
- grad_flat: float32 [5573632], P('dp')
- params_new: float32 [5573632], P('dp')
- moment_one_new: float32 [5573632], P('dp')
- moment_two_new: float32 [5573632], P('dp')
The draws below stay inside these ranges and needn't reach their ends.
Inputs may be any that keep to these rules, and one draw needn't show every extreme that they name: `seq_lengths`: sequences 2j and 2j + 1 go to the same device; on each device their lengths sum to 1 to 128, and sequence 2j has a token or more; one sequence has exactly 128 tokens and its partner has none; other sequences 2j + 1 may have none too. `seq_owner`: each device holds exactly the two sequences 2j and 2j + 1 for one j.
All inputs are finite; a program needn't handle non-finite values.
Results may differ from the reference program's by a relative error of at most 0.012.
The reference program's roundings to bfloat16 on the way count: a program that leaves them out, or rounds other values in their place, can miss the bound.
Values may be sent and summed in bfloat16 or wider, within the bound.
No kernel may reach another device: no remote copies, remote signals or barrier semaphores. Data moves between devices by JAX's collectives and lax.ppermute only.
A program may use at most 128 MiB of HBM per device.

```python
import math
import jax
import jax.numpy as jnp
from jax import lax

D = 640
FF = 2048
HD = 256
HQ = 1024
CAP = 128
WINDOW = 64
STEP = 3
TOKENS = 4096
G1LEN = 1638400
G2LEN = 3932160
G3LEN = 3072
FLAT = 5573632
N_DP = 32


def normal_block(key, entries, fan_in):
    return jax.random.truncated_normal(key, -3.0, 3.0, (entries,), jnp.float32) * fan_in ** (-0.5)


def draw_params(key, part):
    subkeys = jax.random.split(jax.random.fold_in(key, 11), 9)
    attn_group = jnp.concatenate([normal_block(subkeys[0], D * HQ, D), normal_block(subkeys[1], D * HD, D), normal_block(subkeys[2], D * HD, D), normal_block(subkeys[3], HQ * D, HQ) * 2.0])
    ffn_group = jnp.concatenate([normal_block(subkeys[4], D * FF, D), normal_block(subkeys[5], D * FF, D), normal_block(subkeys[6], FF * D, FF)])
    outer_gains = jax.random.uniform(subkeys[7], (4 * D,), jnp.float32, -0.3, 0.3)
    inner_gains = jax.random.uniform(subkeys[8], (2 * HD,), jnp.float32, -0.3, 0.3)
    gain_group = jnp.concatenate([outer_gains[:D], inner_gains, outer_gains[D:]])
    table = jnp.concatenate([attn_group.reshape(N_DP, -1), ffn_group.reshape(N_DP, -1), gain_group.reshape(N_DP, -1)], axis=1)
    return table.reshape(-1)


def pair_draw(key):
    subkeys = jax.random.split(jax.random.fold_in(key, 29), 5)
    pair_index = jnp.arange(N_DP, dtype=jnp.int32)
    radius = jax.random.randint(subkeys[0], (N_DP,), 7, 17)
    summed = jnp.maximum(CAP * radius * radius // 256, 1)
    chosen = jax.random.randint(subkeys[1], (), 0, N_DP)
    summed = jnp.where(pair_index == chosen, CAP, summed)
    divided = jax.random.randint(subkeys[2], (N_DP,), 0, 2)
    divided = jnp.where(pair_index == chosen, 0, divided)
    leading = 1 + jax.random.randint(subkeys[3], (N_DP,), 0, jnp.maximum(summed - 1, 1))
    leading = jnp.where(divided == 1, leading, summed)
    trailing = summed - leading
    lengths = jnp.stack([leading, trailing], axis=1).reshape(-1).astype(jnp.int32)
    owners = jnp.repeat(jax.random.permutation(subkeys[4], N_DP).astype(jnp.int32), 2)
    return (lengths, owners)


def draw_seq_lengths(key, part):
    return pair_draw(key)[0]


def draw_seq_owner(key, part):
    return pair_draw(key)[1]


def levels(stream_key, shape, pieces, low, top_value):
    factor_of = 1.0
    for dim, parts in pieces:
        draws = jax.random.uniform(jax.random.fold_in(jax.random.fold_in(stream_key, 6), dim), (parts,), jnp.float32, low / len(pieces), top_value / len(pieces))
        factor_of = factor_of * jnp.repeat(jnp.exp(draws), shape[dim] // parts).reshape((-1,) + (1,) * (len(shape) - 1 - dim))
    return factor_of


def noise(own_key, extent, spread, reach, shards=(), held_as=jnp.bfloat16):
    drawn = spread * jax.random.normal(own_key, extent, jnp.float32)
    if shards:
        drawn = drawn * levels(own_key, extent, shards, -0.22, 0.18)
    return jnp.clip(drawn, -reach, reach).astype(held_as)


def setup_inputs(seed: int = 0) -> dict:
    key_list = jax.random.split(jax.random.key(seed), 8)
    hidden_in = noise(key_list[0], (TOKENS, D), 1.0, 6.0, ((0, 32),))
    cotangent = noise(key_list[1], (TOKENS, D), 1.0, 6.0, ((0, 32),))
    params = draw_params(jax.random.fold_in(key_list[7], 71), 0)
    moment_one = noise(key_list[3], (FLAT,), 1.5, 6.0, ((0, 32),), jnp.float32)
    moment_two = jnp.clip(jnp.exp(math.log(0.5) - 3.218876 * jax.random.uniform(key_list[4], (FLAT,), jnp.float32) ** levels(key_list[4], (FLAT,), ((0, 32),), -0.2, 0.2)), 0.02, 0.5)
    seq_lengths = draw_seq_lengths(jax.random.fold_in(key_list[7], 71), 0)
    seq_owner = draw_seq_owner(jax.random.fold_in(key_list[7], 71), 0)
    return dict(hidden_in=hidden_in, cotangent=cotangent, params=params, moment_one=moment_one, moment_two=moment_two, seq_lengths=seq_lengths, seq_owner=seq_owner)


def rms_scale(values, gain_vec):
    return values * lax.rsqrt(lax.optimization_barrier(jnp.mean(values * values, axis=-1, keepdims=True)) + 1e-06) * (1.0 + gain_vec)

def rotate(values, cos_tab, sin_tab):
    half_dim = values.shape[-1] // 2
    lower_half = values[..., :half_dim]
    upper_half = values[..., half_dim:]
    return jnp.concatenate([lower_half * cos_tab - upper_half * sin_tab, upper_half * cos_tab + lower_half * sin_tab], axis=-1)

def query_key(query_raw, key_raw, gain_query, gain_key, cos_tab, sin_tab):
    per_head = query_raw.reshape(query_raw.shape[0], -1, HD).transpose(1, 0, 2)
    rot_query = rotate(rms_scale(per_head, gain_query), cos_tab, sin_tab) * HD ** (-0.5)
    rot_key = rotate(rms_scale(key_raw, gain_key), cos_tab, sin_tab)
    return (rot_query, rot_key)

def gated_gelu(gate_proj, up_proj):
    return jax.nn.gelu(gate_proj, approximate=True) * up_proj

def outer_sum(left_side, right_side):
    return lax.dot_general(left_side, right_side, (((0,), (0,)), ((), ())), preferred_element_type=jnp.float32)

def times_transposed(rows_in, matrix):
    return lax.dot_general(rows_in, matrix, (((1,), (1,)), ((), ())), preferred_element_type=jnp.float32)

def slot_setup(seq_lengths, seq_owner, device):
    mine_mask = seq_owner == device
    own_lengths = jnp.where(mine_mask, seq_lengths, 0).astype(jnp.int32)
    seq_ends = jnp.cumsum(own_lengths, dtype=jnp.int32)
    seq_begins = seq_ends - own_lengths
    slot_index = jnp.arange(CAP, dtype=jnp.int32)
    column = slot_index[:, None]
    inside_mask = mine_mask[None, :] & (seq_begins[None, :] <= column) & (column < seq_ends[None, :])
    live_mask = jnp.any(inside_mask, axis=1)
    seq_label = lax.optimization_barrier(jnp.sum((mine_mask[None, :] & (seq_ends[None, :] <= column)).astype(jnp.int32), axis=1, dtype=jnp.int32))
    position = lax.optimization_barrier(jnp.sum(jnp.where(inside_mask, column - seq_begins[None, :], 0), axis=1, dtype=jnp.int32))
    row_slot = slot_index[:, None]
    col_slot = slot_index[None, :]
    allowed = live_mask[:, None] & live_mask[None, :] & (seq_label[:, None] == seq_label[None, :]) & (col_slot <= row_slot) & (row_slot - col_slot < WINDOW) | (row_slot == col_slot)
    half_dim = HD // 2
    frequency = 10000.0 ** (-2.0 * jnp.arange(half_dim, dtype=jnp.float32) / HD)
    angles = position.astype(jnp.float32)[:, None] * frequency[None, :]
    return (live_mask.astype(jnp.float32), allowed, jnp.cos(angles), jnp.sin(angles))

def attend(rot_query, rot_key, value_vec, allowed):
    num_heads = rot_query.shape[0]
    num_slots = rot_key.shape[0]
    flat_query = rot_query.reshape(num_heads * num_slots, HD)
    scores = lax.dot_general(flat_query, rot_key, (((1,), (1,)), ((), ())), preferred_element_type=jnp.float32)
    scores = jnp.where(allowed[None], scores.reshape(num_heads, num_slots, num_slots), -1e+30)
    row_max = lax.optimization_barrier(jnp.max(scores, axis=-1, keepdims=True))
    raised = jnp.exp(scores - row_max)
    summed = lax.optimization_barrier(jnp.sum(raised, axis=-1, keepdims=True))
    log_total = row_max + jnp.log(summed)
    attn_prob = (raised / summed).astype(jnp.bfloat16)
    context = jnp.dot(attn_prob.reshape(num_heads * num_slots, num_slots), value_vec, preferred_element_type=jnp.float32)
    context = context.reshape(num_heads, num_slots, HD).transpose(1, 0, 2).reshape(num_slots, num_heads * HD)
    return (context.astype(jnp.bfloat16), log_total)

def attend_back(rot_query, rot_key, value_vec, allowed, log_total, context, delta_context):
    num_heads = rot_query.shape[0]
    num_slots = rot_key.shape[0]
    head_delta = delta_context.reshape(num_slots, num_heads, HD).transpose(1, 0, 2).reshape(-1, HD)
    head_context = context.reshape(num_slots, num_heads, HD).transpose(1, 0, 2).reshape(-1, HD)
    row_dot = lax.optimization_barrier(jnp.sum(head_delta.astype(jnp.float32) * head_context.astype(jnp.float32), axis=-1, keepdims=True))
    flat_query = rot_query.reshape(-1, HD)
    scores = lax.dot_general(flat_query, rot_key, (((1,), (1,)), ((), ())), preferred_element_type=jnp.float32)
    scores = jnp.where(allowed[None], scores.reshape(num_heads, num_slots, num_slots), -1e+30)
    prob_exact = jnp.exp(scores - log_total).reshape(-1, num_slots)
    delta_value = lax.dot_general(prob_exact.astype(jnp.bfloat16), head_delta, (((0,), (0,)), ((), ())), preferred_element_type=jnp.float32)
    delta_prob = lax.dot_general(head_delta, value_vec, (((1,), (1,)), ((), ())), preferred_element_type=jnp.float32)
    delta_score = (prob_exact * (delta_prob - row_dot)).astype(jnp.bfloat16)
    delta_query = jnp.dot(delta_score, rot_key, preferred_element_type=jnp.float32).reshape(num_heads, num_slots, HD)
    delta_key = lax.dot_general(delta_score, flat_query, (((0,), (0,)), ((), ())), preferred_element_type=jnp.float32)
    return (delta_query, delta_key, delta_value.astype(jnp.bfloat16))

def split_groups(flat_vec, devices):
    table = flat_vec.reshape(devices, -1)
    attn_len = G1LEN // devices
    ffn_len = G2LEN // devices
    return (table[:, :attn_len].reshape(-1), table[:, attn_len:attn_len + ffn_len].reshape(-1), table[:, attn_len + ffn_len:].reshape(-1))

def join_groups(groups, devices):
    return jnp.concatenate([member.reshape(devices, -1) for member in groups], axis=1).reshape(-1)

def flat_join(arrays):
    return jnp.concatenate([member.reshape(-1) for member in arrays])

def unpack_weights(attn_flat, ffn_flat, gain_flat):
    cut_query = D * HQ
    cut_key = cut_query + D * HD
    cut_value = cut_key + D * HD
    query_weight = attn_flat[:cut_query].reshape(D, HQ)
    key_weight = attn_flat[cut_query:cut_key].reshape(D, HD)
    value_weight = attn_flat[cut_key:cut_value].reshape(D, HD)
    out_weight = attn_flat[cut_value:].reshape(HQ, D)
    cut_gate = D * FF
    gate_weight = ffn_flat[:cut_gate].reshape(D, FF)
    up_weight = ffn_flat[cut_gate:2 * cut_gate].reshape(D, FF)
    down_weight = ffn_flat[2 * cut_gate:].reshape(FF, D)
    gains = gain_flat.astype(jnp.float32)
    gain_set = (gains[:D], gains[D:D + HD], gains[D + HD:D + 2 * HD], gains[D + 2 * HD:2 * D + 2 * HD], gains[2 * D + 2 * HD:3 * D + 2 * HD], gains[3 * D + 2 * HD:])
    return (query_weight, key_weight, value_weight, out_weight, gate_weight, up_weight, down_weight, gain_set)

def forward_pass(input_rows, weights, allowed, cos_tab, sin_tab):
    query_weight, key_weight, value_weight, out_weight, gate_weight, up_weight, down_weight, gain_set = weights
    gain_in, gain_query, gain_key, gain_post, gain_mid, gain_last = gain_set
    resid_in = input_rows.astype(jnp.float32)
    normed_in = rms_scale(resid_in, gain_in).astype(jnp.bfloat16)
    query_raw = jnp.dot(normed_in, query_weight, preferred_element_type=jnp.float32)
    key_raw = jnp.dot(normed_in, key_weight, preferred_element_type=jnp.float32)
    value_vec = jnp.dot(normed_in, value_weight, preferred_element_type=jnp.float32).astype(jnp.bfloat16)
    rot_query, rot_key = query_key(query_raw, key_raw, gain_query, gain_key, cos_tab, sin_tab)
    rot_query = rot_query.astype(jnp.bfloat16)
    rot_key = rot_key.astype(jnp.bfloat16)
    context, log_total = attend(rot_query, rot_key, value_vec, allowed)
    attn_out = jnp.dot(context, out_weight, preferred_element_type=jnp.float32)
    mid_stream = resid_in + rms_scale(attn_out, gain_post)
    normed_mid = rms_scale(mid_stream, gain_mid).astype(jnp.bfloat16)
    gate_proj = jnp.dot(normed_mid, gate_weight, preferred_element_type=jnp.float32)
    up_proj = jnp.dot(normed_mid, up_weight, preferred_element_type=jnp.float32)
    hidden = gated_gelu(gate_proj, up_proj).astype(jnp.bfloat16)
    ffn_out = jnp.dot(hidden, down_weight, preferred_element_type=jnp.float32)
    block_out = (mid_stream + rms_scale(ffn_out, gain_last)).astype(jnp.bfloat16)
    saved = (resid_in, normed_in, query_raw, key_raw, value_vec, rot_query, rot_key, context, log_total, attn_out, mid_stream, normed_mid, gate_proj, up_proj, hidden, ffn_out)
    return (block_out, saved)

def ffn_backward(cot_rows, live_mask, weights, saved):
    gate_weight, up_weight, down_weight, gain_set = (weights[4], weights[5], weights[6], weights[7])
    gain_mid, gain_last = (gain_set[4], gain_set[5])
    mid_stream, normed_mid, gate_proj, up_proj, hidden, ffn_out = saved[10:]
    delta_out = cot_rows.astype(jnp.float32) * live_mask[:, None]
    unused, pullback = jax.vjp(rms_scale, ffn_out, gain_last)
    delta_ffn, gain_last_grad = pullback(delta_out)
    delta_ffn = delta_ffn.astype(jnp.bfloat16)
    down_grad = outer_sum(hidden, delta_ffn)
    delta_hidden = times_transposed(delta_ffn, down_weight)
    unused, pullback = jax.vjp(gated_gelu, gate_proj, up_proj)
    delta_gate, delta_up = pullback(delta_hidden)
    delta_gate = delta_gate.astype(jnp.bfloat16)
    delta_up = delta_up.astype(jnp.bfloat16)
    gate_grad = outer_sum(normed_mid, delta_gate)
    up_grad = outer_sum(normed_mid, delta_up)
    delta_normed = times_transposed(delta_gate, gate_weight) + times_transposed(delta_up, up_weight)
    unused, pullback = jax.vjp(rms_scale, mid_stream, gain_mid)
    delta_part, gain_mid_grad = pullback(delta_normed)
    delta_mid = delta_out + delta_part
    return (delta_mid, (gate_grad, up_grad, down_grad), (gain_mid_grad, gain_last_grad))

def attn_backward(delta_mid, weights, saved, allowed, cos_tab, sin_tab):
    query_weight, key_weight, value_weight, out_weight = weights[:4]
    gain_in, gain_query, gain_key, gain_post = weights[7][:4]
    resid_in, normed_in, query_raw, key_raw, value_vec, rot_query, rot_key, context, log_total, attn_out = saved[:10]
    unused, pullback = jax.vjp(rms_scale, attn_out, gain_post)
    delta_attn, gain_post_grad = pullback(delta_mid)
    delta_attn = delta_attn.astype(jnp.bfloat16)
    out_grad = outer_sum(context, delta_attn)
    delta_context = times_transposed(delta_attn, out_weight).astype(jnp.bfloat16)
    delta_query, delta_key, delta_value = attend_back(rot_query, rot_key, value_vec, allowed, log_total, context, delta_context)

    def rope_map(raw_query, raw_key, query_gain, key_gain):
        return query_key(raw_query, raw_key, query_gain, key_gain, cos_tab, sin_tab)
    unused, pullback = jax.vjp(rope_map, query_raw, key_raw, gain_query, gain_key)
    delta_qraw, delta_kraw, gain_query_grad, gain_key_grad = pullback((delta_query, delta_key))
    delta_qraw = delta_qraw.astype(jnp.bfloat16)
    delta_kraw = delta_kraw.astype(jnp.bfloat16)
    query_grad = outer_sum(normed_in, delta_qraw)
    key_grad = outer_sum(normed_in, delta_kraw)
    value_grad = outer_sum(normed_in, delta_value)
    delta_in = times_transposed(delta_qraw, query_weight) + times_transposed(delta_kraw, key_weight) + times_transposed(delta_value, value_weight)
    unused, pullback = jax.vjp(rms_scale, resid_in, gain_in)
    delta_part, gain_in_grad = pullback(delta_in)
    grad_in = delta_mid + delta_part
    return (grad_in, (query_grad, key_grad, value_grad, out_grad), (gain_in_grad, gain_query_grad, gain_key_grad, gain_post_grad))

def adam_update(weight_shard, gradient, moment_one, moment_two):
    moment_one = 0.9 * moment_one + 0.1 * gradient
    moment_two = 0.999 * moment_two + 0.001 * gradient * gradient
    fix_one = 1.0 - 0.9 ** STEP
    fix_two = 1.0 - 0.999 ** STEP
    weight_shard = weight_shard - 0.02 * (moment_one / fix_one / (jnp.sqrt(moment_two / fix_two) + 1e-08) + 0.1 * weight_shard)
    return (weight_shard, moment_one, moment_two)

def reference(hidden_in, cotangent, params, moment_one, moment_two, seq_lengths, seq_owner):
    weights = unpack_weights(*split_groups(params.astype(jnp.bfloat16), N_DP))

    def one_block(running, block_item):
        input_rows, cot_rows, device = block_item
        live_mask, allowed, cos_tab, sin_tab = slot_setup(seq_lengths, seq_owner, device)
        block_out, saved = forward_pass(input_rows, weights, allowed, cos_tab, sin_tab)
        delta_mid, ffn_grads, late_gains = ffn_backward(cot_rows, live_mask, weights, saved)
        grad_in, attn_grads, early_gains = attn_backward(delta_mid, weights, saved, allowed, cos_tab, sin_tab)
        groups = (flat_join(attn_grads), flat_join(ffn_grads), flat_join(early_gains + late_gains))
        return (tuple((total + term for total, term in zip(running, groups))), (block_out, grad_in))
    zeros = (jnp.zeros((G1LEN,), jnp.float32), jnp.zeros((G2LEN,), jnp.float32), jnp.zeros((G3LEN,), jnp.float32))
    items = (hidden_in.reshape(N_DP, CAP, D), cotangent.reshape(N_DP, CAP, D), jnp.arange(N_DP, dtype=jnp.int32))
    groups, (outputs, input_grads) = lax.scan(one_block, zeros, items)
    grad_flat = join_groups(groups, N_DP)
    params_new, moment_one_new, moment_two_new = adam_update(params, grad_flat, moment_one, moment_two)
    return (outputs.reshape(TOKENS, D), input_grads.reshape(TOKENS, D), grad_flat, params_new, moment_one_new, moment_two_new)
```

```python
import jax
import jax.numpy as jnp
from jax import lax
from jax.sharding import PartitionSpec as P

D = 640
FF = 2048
HD = 256
HQ = 1024
CAP = 128
WINDOW = 64
STEP = 3
G1LEN = 1638400
G2LEN = 3932160
LANE_BLOCK = 1024
SEND = jnp.bfloat16


def rms_scale(values, gain_vec):
    return (
        values
        * lax.rsqrt(jnp.mean(values * values, axis=-1, keepdims=True) + 1e-06)
        * (1.0 + gain_vec)
    )


def rotate(values, cos_tab, sin_tab):
    half_dim = values.shape[-1] // 2
    lower_half = values[..., :half_dim]
    upper_half = values[..., half_dim:]
    return jnp.concatenate(
        [lower_half * cos_tab - upper_half * sin_tab, upper_half * cos_tab + lower_half * sin_tab],
        axis=-1,
    )


def query_key(query_raw, key_raw, gain_query, gain_key, cos_tab, sin_tab):
    per_head = query_raw.reshape(query_raw.shape[0], -1, HD).transpose(1, 0, 2)
    rot_query = rotate(rms_scale(per_head, gain_query), cos_tab, sin_tab) * HD ** (-0.5)
    rot_key = rotate(rms_scale(key_raw, gain_key), cos_tab, sin_tab)
    return (rot_query, rot_key)


def gated_gelu(gate_proj, up_proj):
    return jax.nn.gelu(gate_proj, approximate=True) * up_proj


def outer_sum(left_side, right_side):
    return lax.dot_general(
        left_side, right_side, (((0,), (0,)), ((), ())), preferred_element_type=jnp.float32
    )


def times_transposed(rows_in, matrix):
    return lax.dot_general(
        rows_in, matrix, (((1,), (1,)), ((), ())), preferred_element_type=jnp.float32
    )


def slot_setup(seq_lengths, seq_owner, device):
    mine_mask = seq_owner == device
    own_lengths = jnp.where(mine_mask, seq_lengths, 0)
    seq_ends = jnp.cumsum(own_lengths, dtype=jnp.int32)
    seq_begins = seq_ends - own_lengths
    slot_index = jnp.arange(CAP, dtype=jnp.int32)
    column = slot_index[:, None]
    inside_mask = (
        mine_mask[None, :] & (seq_begins[None, :] <= column) & (column < seq_ends[None, :])
    )
    live_mask = jnp.any(inside_mask, axis=1)
    seq_label = jnp.sum(
        (mine_mask[None, :] & (seq_ends[None, :] <= column)).astype(jnp.int32),
        axis=1,
        dtype=jnp.int32,
    )
    position = jnp.sum(
        jnp.where(inside_mask, column - seq_begins[None, :], 0), axis=1, dtype=jnp.int32
    )
    row_slot = slot_index[:, None]
    col_slot = slot_index[None, :]
    allowed = live_mask[:, None] & live_mask[None, :] & (
        seq_label[:, None] == seq_label[None, :]
    ) & (col_slot <= row_slot) & (row_slot - col_slot < WINDOW) | (row_slot == col_slot)
    half_dim = HD // 2
    frequency = 10000.0 ** (-2.0 * jnp.arange(half_dim, dtype=jnp.float32) / HD)
    angles = position.astype(jnp.float32)[:, None] * frequency[None, :]
    return (live_mask.astype(jnp.float32), allowed, jnp.cos(angles), jnp.sin(angles))


def attend(rot_query, rot_key, value_vec, allowed):
    num_heads = rot_query.shape[0]
    num_slots = rot_key.shape[0]
    flat_query = rot_query.reshape(num_heads * num_slots, HD)
    scores = lax.dot_general(
        flat_query, rot_key, (((1,), (1,)), ((), ())), preferred_element_type=jnp.float32
    )
    scores = jnp.where(allowed[None], scores.reshape(num_heads, num_slots, num_slots), -1e30)
    row_max = jnp.max(scores, axis=-1, keepdims=True)
    raised = jnp.exp(scores - row_max)
    summed = jnp.sum(raised, axis=-1, keepdims=True)
    log_total = row_max + jnp.log(summed)
    attn_prob = (raised / summed).astype(jnp.bfloat16)
    context = jnp.dot(
        attn_prob.reshape(num_heads * num_slots, num_slots),
        value_vec,
        preferred_element_type=jnp.float32,
    )
    context = (
        context.reshape(num_heads, num_slots, HD)
        .transpose(1, 0, 2)
        .reshape(num_slots, num_heads * HD)
    )
    return (context.astype(jnp.bfloat16), log_total)


def attend_back(rot_query, rot_key, value_vec, allowed, log_total, context, delta_context):
    num_heads = rot_query.shape[0]
    num_slots = rot_key.shape[0]
    head_delta = delta_context.reshape(num_slots, num_heads, HD).transpose(1, 0, 2).reshape(-1, HD)
    head_context = context.reshape(num_slots, num_heads, HD).transpose(1, 0, 2).reshape(-1, HD)
    row_dot = jnp.sum(
        head_delta.astype(jnp.float32) * head_context.astype(jnp.float32), axis=-1, keepdims=True
    )
    flat_query = rot_query.reshape(-1, HD)
    scores = lax.dot_general(
        flat_query, rot_key, (((1,), (1,)), ((), ())), preferred_element_type=jnp.float32
    )
    scores = jnp.where(allowed[None], scores.reshape(num_heads, num_slots, num_slots), -1e30)
    prob_exact = jnp.exp(scores - log_total).reshape(-1, num_slots)
    delta_value = lax.dot_general(
        prob_exact.astype(jnp.bfloat16),
        head_delta,
        (((0,), (0,)), ((), ())),
        preferred_element_type=jnp.float32,
    )
    delta_prob = lax.dot_general(
        head_delta, value_vec, (((1,), (1,)), ((), ())), preferred_element_type=jnp.float32
    )
    delta_score = (prob_exact * (delta_prob - row_dot)).astype(jnp.bfloat16)
    delta_query = jnp.dot(delta_score, rot_key, preferred_element_type=jnp.float32).reshape(
        num_heads, num_slots, HD
    )
    delta_key = lax.dot_general(
        delta_score, flat_query, (((0,), (0,)), ((), ())), preferred_element_type=jnp.float32
    )
    return (delta_query, delta_key, delta_value.astype(jnp.bfloat16))


def flat_table(arrays, devices):
    return jnp.concatenate([member.reshape(-1) for member in arrays]).reshape(devices, -1)


def unpack_weights(attn_flat, ffn_flat, gain_flat):
    cut_query = D * HQ
    cut_key = cut_query + D * HD
    cut_value = cut_key + D * HD
    query_weight = attn_flat[:cut_query].reshape(D, HQ)
    key_weight = attn_flat[cut_query:cut_key].reshape(D, HD)
    value_weight = attn_flat[cut_key:cut_value].reshape(D, HD)
    out_weight = attn_flat[cut_value:].reshape(HQ, D)
    cut_gate = D * FF
    gate_weight = ffn_flat[:cut_gate].reshape(D, FF)
    up_weight = ffn_flat[cut_gate : 2 * cut_gate].reshape(D, FF)
    down_weight = ffn_flat[2 * cut_gate :].reshape(FF, D)
    gains = gain_flat.astype(jnp.float32)
    gain_set = (
        gains[:D],
        gains[D : D + HD],
        gains[D + HD : D + 2 * HD],
        gains[D + 2 * HD : 2 * D + 2 * HD],
        gains[2 * D + 2 * HD : 3 * D + 2 * HD],
        gains[3 * D + 2 * HD :],
    )
    return (
        query_weight,
        key_weight,
        value_weight,
        out_weight,
        gate_weight,
        up_weight,
        down_weight,
        gain_set,
    )


def forward_pass(input_rows, weights, allowed, cos_tab, sin_tab):
    (
        query_weight,
        key_weight,
        value_weight,
        out_weight,
        gate_weight,
        up_weight,
        down_weight,
        gain_set,
    ) = weights
    gain_in, gain_query, gain_key, gain_post, gain_mid, gain_last = gain_set
    resid_in = input_rows.astype(jnp.float32)
    normed_in = rms_scale(resid_in, gain_in).astype(jnp.bfloat16)
    query_raw = jnp.dot(normed_in, query_weight, preferred_element_type=jnp.float32)
    key_raw = jnp.dot(normed_in, key_weight, preferred_element_type=jnp.float32)
    value_vec = jnp.dot(normed_in, value_weight, preferred_element_type=jnp.float32).astype(
        jnp.bfloat16
    )
    rot_query, rot_key = query_key(query_raw, key_raw, gain_query, gain_key, cos_tab, sin_tab)
    rot_query = rot_query.astype(jnp.bfloat16)
    rot_key = rot_key.astype(jnp.bfloat16)
    context, log_total = attend(rot_query, rot_key, value_vec, allowed)
    attn_out = jnp.dot(context, out_weight, preferred_element_type=jnp.float32)
    mid_stream = resid_in + rms_scale(attn_out, gain_post)
    normed_mid = rms_scale(mid_stream, gain_mid).astype(jnp.bfloat16)
    gate_proj = jnp.dot(normed_mid, gate_weight, preferred_element_type=jnp.float32)
    up_proj = jnp.dot(normed_mid, up_weight, preferred_element_type=jnp.float32)
    hidden = gated_gelu(gate_proj, up_proj).astype(jnp.bfloat16)
    ffn_out = jnp.dot(hidden, down_weight, preferred_element_type=jnp.float32)
    block_out = (mid_stream + rms_scale(ffn_out, gain_last)).astype(jnp.bfloat16)
    saved = (
        resid_in,
        normed_in,
        query_raw,
        key_raw,
        value_vec,
        rot_query,
        rot_key,
        context,
        log_total,
        attn_out,
        mid_stream,
        normed_mid,
        gate_proj,
        up_proj,
        hidden,
        ffn_out,
    )
    return (block_out, saved)


def ffn_backward(cot_rows, live_mask, weights, saved):
    gate_weight, up_weight, down_weight, gain_set = (weights[4], weights[5], weights[6], weights[7])
    gain_mid, gain_last = (gain_set[4], gain_set[5])
    mid_stream, normed_mid, gate_proj, up_proj, hidden, ffn_out = saved[10:]
    delta_out = cot_rows.astype(jnp.float32) * live_mask[:, None]
    unused, pullback = jax.vjp(rms_scale, ffn_out, gain_last)
    delta_ffn, gain_last_grad = pullback(delta_out)
    delta_ffn = delta_ffn.astype(jnp.bfloat16)
    down_grad = outer_sum(hidden, delta_ffn)
    delta_hidden = times_transposed(delta_ffn, down_weight)
    unused, pullback = jax.vjp(gated_gelu, gate_proj, up_proj)
    delta_gate, delta_up = pullback(delta_hidden)
    delta_gate = delta_gate.astype(jnp.bfloat16)
    delta_up = delta_up.astype(jnp.bfloat16)
    gate_grad = outer_sum(normed_mid, delta_gate)
    up_grad = outer_sum(normed_mid, delta_up)
    delta_normed = times_transposed(delta_gate, gate_weight) + times_transposed(delta_up, up_weight)
    unused, pullback = jax.vjp(rms_scale, mid_stream, gain_mid)
    delta_part, gain_mid_grad = pullback(delta_normed)
    delta_mid = delta_out + delta_part
    return (delta_mid, (gate_grad, up_grad, down_grad), (gain_mid_grad, gain_last_grad))


def attn_backward(delta_mid, weights, saved, allowed, cos_tab, sin_tab):
    query_weight, key_weight, value_weight, out_weight = weights[:4]
    gain_in, gain_query, gain_key, gain_post = weights[7][:4]
    (
        resid_in,
        normed_in,
        query_raw,
        key_raw,
        value_vec,
        rot_query,
        rot_key,
        context,
        log_total,
        attn_out,
    ) = saved[:10]
    unused, pullback = jax.vjp(rms_scale, attn_out, gain_post)
    delta_attn, gain_post_grad = pullback(delta_mid)
    delta_attn = delta_attn.astype(jnp.bfloat16)
    out_grad = outer_sum(context, delta_attn)
    delta_context = times_transposed(delta_attn, out_weight).astype(jnp.bfloat16)
    delta_query, delta_key, delta_value = attend_back(
        rot_query, rot_key, value_vec, allowed, log_total, context, delta_context
    )

    def rope_map(raw_query, raw_key, query_gain, key_gain):
        return query_key(raw_query, raw_key, query_gain, key_gain, cos_tab, sin_tab)

    unused, pullback = jax.vjp(rope_map, query_raw, key_raw, gain_query, gain_key)
    delta_qraw, delta_kraw, gain_query_grad, gain_key_grad = pullback((delta_query, delta_key))
    delta_qraw = delta_qraw.astype(jnp.bfloat16)
    delta_kraw = delta_kraw.astype(jnp.bfloat16)
    query_grad = outer_sum(normed_in, delta_qraw)
    key_grad = outer_sum(normed_in, delta_kraw)
    value_grad = outer_sum(normed_in, delta_value)
    delta_in = (
        times_transposed(delta_qraw, query_weight)
        + times_transposed(delta_kraw, key_weight)
        + times_transposed(delta_value, value_weight)
    )
    unused, pullback = jax.vjp(rms_scale, resid_in, gain_in)
    delta_part, gain_in_grad = pullback(delta_in)
    grad_in = delta_mid + delta_part
    return (
        grad_in,
        (query_grad, key_grad, value_grad, out_grad),
        (gain_in_grad, gain_query_grad, gain_key_grad, gain_post_grad),
    )


def adam_update(weight_shard, gradient, moment_one, moment_two):
    moment_one = 0.9 * moment_one + 0.1 * gradient
    moment_two = 0.999 * moment_two + 0.001 * gradient * gradient
    fix_one = 1.0 - 0.9**STEP
    fix_two = 1.0 - 0.999**STEP
    weight_shard = weight_shard - 0.02 * (
        moment_one / fix_one / (jnp.sqrt(moment_two / fix_two) + 1e-08) + 0.1 * weight_shard
    )
    return (weight_shard, moment_one, moment_two)


def padded_length(entries):
    return -(-entries // LANE_BLOCK) * LANE_BLOCK


def per_device(hidden_in, cotangent, params, moment_one, moment_two, seq_lengths, seq_owner):
    devices = lax.axis_size("dp")
    attn_len = G1LEN // devices
    ffn_len = G2LEN // devices
    gain_len = params.shape[0] - attn_len - ffn_len
    small_len = attn_len + gain_len
    pad_len = padded_length(small_len) - small_len
    rounded = params.astype(jnp.bfloat16)
    first_part = jnp.concatenate(
        [rounded[:attn_len], rounded[attn_len + ffn_len :], jnp.zeros((pad_len,), jnp.bfloat16)]
    )
    first_table = lax.all_gather(first_part, "dp", axis=0, tiled=True).reshape(devices, -1)
    attn_flat = first_table[:, :attn_len].reshape(-1)
    gain_flat = first_table[:, attn_len:small_len].reshape(-1)
    ffn_flat = lax.all_gather(rounded[attn_len : attn_len + ffn_len], "dp", axis=0, tiled=True)
    weights = unpack_weights(attn_flat, ffn_flat, gain_flat)
    device = lax.axis_index("dp")
    live_mask, allowed, cos_tab, sin_tab = slot_setup(seq_lengths, seq_owner, device)
    block_out, saved = forward_pass(hidden_in, weights, allowed, cos_tab, sin_tab)
    delta_mid, ffn_grads, late_gains = ffn_backward(cotangent, live_mask, weights, saved)
    ffn_group = jnp.concatenate([member.astype(SEND).reshape(-1) for member in ffn_grads])
    ffn_shard = lax.psum_scatter(ffn_group, "dp", scatter_dimension=0, tiled=True)
    grad_in, attn_grads, early_gains = attn_backward(
        delta_mid, weights, saved, allowed, cos_tab, sin_tab
    )
    attn_group = flat_table([member.astype(SEND) for member in attn_grads], devices)
    gain_group = flat_table(
        [member.astype(SEND) for member in early_gains + late_gains], devices
    )
    small_group = jnp.concatenate(
        [attn_group, gain_group, jnp.zeros((devices, pad_len), SEND)], axis=1
    ).reshape(-1)
    small_shard = lax.psum_scatter(small_group, "dp", scatter_dimension=0, tiled=True)
    grad_shard = jnp.concatenate(
        [small_shard[:attn_len], ffn_shard, small_shard[attn_len:small_len]]
    ).astype(jnp.float32)
    params_new, moment_one_new, moment_two_new = adam_update(
        params, grad_shard, moment_one, moment_two
    )
    return (block_out, grad_in, grad_shard, params_new, moment_one_new, moment_two_new)


def solution(mesh):
    in_specs = (P("dp", None), P("dp", None), P("dp"), P("dp"), P("dp"), P(), P())
    out_specs = (P("dp", None), P("dp", None), P("dp"), P("dp"), P("dp"), P("dp"))
    return jax.shard_map(
        per_device, mesh=mesh, in_specs=in_specs, out_specs=out_specs, check_vma=False
    )
```
